32 devices in a mesh: groups: 2 (over y), seq: 8 (over z, x), tensor: 2 (over core).
Axes of the slice: x: 2, y: 2, z: 4, core: 2. Of those that a mesh axis runs over, the one named last changes fastest.
Arguments:
- queries: bfloat16 [256, 3072], P(('groups', 'seq'), 'tensor'), parts along dimension 0, may hold values from -8 to 8
- keys: bfloat16 [16384, 3072], P(('groups', 'seq'), 'tensor'), parts along dimension 0, may hold values from -8 to 8
- values: bfloat16 [16384, 3072], P(('groups', 'seq'), 'tensor'), parts along dimension 0, may hold values from -6 to 6
Outputs:
- context: bfloat16 [256, 3072], P(('groups', 'seq'), 'tensor'), parts along dimension 0
The draws below stay inside these ranges and needn't reach their ends.
There are 2 independent parts, one for each index of `groups`. The reference program is written for one: setup_inputs(seed, part) draws one part's arguments, and reference() takes and returns one part's arrays. A program takes and returns all parts, laid end to end along the dimension named above; each array names one. Nothing has to cross between parts.
All inputs are finite; a program needn't handle non-finite values.
Results may differ from the reference program's by a relative error of at most 0.0029.
Values may be sent and summed in bfloat16 or wider, within the bound.
A program may use at most 64 MiB of HBM per device.

```python
import math
import jax
import jax.numpy as jnp
from jax import lax

HEADS = 12
HEAD_DIM = 256
KEYS_DEV = 1024
QUERIES = 128
KEYS = 8192
ATTN_WIDTH = 3072
N_SEQ = 8


def drawn_pair(key):
    total_keys = KEYS_DEV * N_SEQ
    columns = HEADS * HEAD_DIM
    query_seed = jax.random.fold_in(key, 11)
    key_seed = jax.random.fold_in(key, 23)
    query_vals = jnp.clip(2.0 * jax.random.normal(query_seed, (QUERIES, columns), jnp.float32), -8.0, 8.0)
    key_vals = jnp.clip(2.0 * jax.random.normal(key_seed, (total_keys, columns), jnp.float32), -8.0, 8.0)
    return (query_vals, key_vals)


def draw_queries(key, part):
    return drawn_pair(key)[0].astype(jnp.bfloat16)


def draw_keys(key, part):
    return drawn_pair(key)[1].astype(jnp.bfloat16)


def steps_of(key, dims, split, low, top_value):
    level, own = 1.0, jax.random.fold_in(key, 6)
    for position, parts in split:
        steps = jnp.exp(jax.random.uniform(jax.random.fold_in(own, position), (parts,), jnp.float32, low / len(split), top_value / len(split)))
        level = level * jnp.repeat(steps, dims[position] // parts).reshape([-1 if axis == position else 1 for axis in range(len(dims))])
    return level


def centred(key, dims, deviation, most, shards=(), dtype=jnp.bfloat16):
    level = steps_of(key, dims, shards, -0.22, 0.18) if shards else 1.0
    entries = jax.random.normal(key, dims, jnp.float32) * deviation * level
    return jnp.minimum(jnp.maximum(entries, -most), most).astype(dtype)


def setup_inputs(seed: int = 0, part: int = 0) -> dict:
    splits = jax.random.split(jax.random.key(seed), 4)
    own_keys = jax.random.split(jax.random.fold_in(splits[3], part), 4)
    queries = draw_queries(jax.random.fold_in(jax.random.fold_in(splits[3], part), 71), part)
    keys = draw_keys(jax.random.fold_in(jax.random.fold_in(splits[3], part), 71), part)
    values = centred(own_keys[2], (KEYS, ATTN_WIDTH), 1.0, 6.0, ((0, 8), (1, 2)))
    return {"queries": queries, "keys": keys, "values": values}


def reference(queries, keys, values):
    query_count = queries.shape[0]
    score_factor = 1.0 / math.sqrt(HEAD_DIM)
    query_heads = queries.astype(jnp.float32).reshape(query_count, HEADS, HEAD_DIM)
    key_blocks = keys.reshape(N_SEQ, KEYS_DEV, HEADS, HEAD_DIM)
    value_blocks = values.reshape(N_SEQ, KEYS_DEV, HEADS, HEAD_DIM)

    def visit_block(carried, block_pair):
        overall, numerator, denominator = carried
        key_block, value_block = block_pair
        scores = jnp.einsum('qhd,khd->qhk', query_heads, key_block.astype(jnp.float32)) * score_factor
        block_peak = lax.optimization_barrier(jnp.max(scores, axis=-1))
        weights = jnp.exp(scores - block_peak[..., None])
        rounded = lax.optimization_barrier(weights.astype(jnp.bfloat16)).astype(jnp.float32)
        block_sums = lax.optimization_barrier(jnp.sum(weights, axis=-1))
        block_context = jnp.einsum('qhk,khd->qhd', rounded, value_block.astype(jnp.float32))
        updated = jnp.maximum(overall, block_peak)
        shrink = jnp.exp(overall - updated)
        stretch = jnp.exp(block_peak - updated)
        numerator = numerator * shrink[..., None] + block_context * stretch[..., None]
        denominator = denominator * shrink + block_sums * stretch
        return ((updated, numerator, denominator), None)
    start = (jnp.full((query_count, HEADS), -1e+30, jnp.float32), jnp.zeros((query_count, HEADS, HEAD_DIM), jnp.float32), jnp.zeros((query_count, HEADS), jnp.float32))
    finished, _ = lax.scan(visit_block, start, (key_blocks, value_blocks))
    numerator = finished[1]
    denominator = finished[2]
    return (numerator / denominator[..., None]).reshape(query_count, HEADS * HEAD_DIM).astype(jnp.bfloat16)
```

```python
import functools
import math

import jax
import jax.numpy as jnp
from jax import lax
from jax.experimental import pallas as pl
from jax.experimental.pallas import tpu as pltpu
from jax.sharding import PartitionSpec as P

HEAD_DIM = 256
LANES = 128
LINK = jnp.bfloat16
SIZES = (2, 2, 2)
QUAD = 4
NEAR = (1, 3, 2)
RAISE = 2.0**60
LOWER = 2.0**-60


def encode(x):
    x = x * RAISE
    return (x * jnp.abs(x)).astype(LINK)


def decode(y):
    y = y.astype(jnp.float32)
    root = jnp.sqrt(jnp.abs(y)) * LOWER
    return jnp.where(y < 0, -root, root)


def over(start, stop, step):
    if stop - start <= 16:
        for index in range(start, stop):
            step(index)
    else:
        lax.fori_loop(start, stop, lambda index, _: (step(index), 0)[1], 0)


def split_heads(heads):
    return SIZES if sum(SIZES) == heads else (heads,)


def kernel(
    n, q_hbm, k_hbm, v_hbm, o_ref, qall, kbuf, vbuf, local, stat, out, xin, zout, zin,
    tout, tin, zstat, ystat,
    own_sem, ksem, vsem, ns, nr, fs, fr, rs, rr, xs, xr, ts, tr, zs, zr, ys, yr,
):
    rows, columns = q_hbm.shape
    heads = columns // HEAD_DIM
    sizes = split_heads(heads)
    starts = [sum(sizes[:c]) for c in range(len(sizes))]
    chunks = len(sizes)
    factor = 1.0 / math.sqrt(HEAD_DIM)
    quads = n // QUAD
    me = lax.axis_index("seq")
    quad = me // QUAD
    place = lax.rem(me, QUAD)

    def heads_of(c):
        return range(starts[c], starts[c] + sizes[c])

    def cols(h):
        return pl.ds(h * HEAD_DIM, HEAD_DIM)

    def span(c):
        return pl.ds(starts[c] * HEAD_DIM, sizes[c] * HEAD_DIM)

    def next_place(j):
        return lax.rem(place + j, QUAD)

    def next_quad(i):
        return lax.rem(quad + i, quads)

    def last_quad(i):
        return lax.rem(quad + quads - i, quads)

    def near(j):
        return quad * QUAD + next_place(j)

    def far(i):
        return next_quad(i) * QUAD + place

    def k_copy(h):
        return pltpu.make_async_copy(k_hbm.at[:, cols(h)], kbuf.at[h], ksem.at[h])

    def v_copy(h):
        return pltpu.make_async_copy(v_hbm.at[:, cols(h)], vbuf.at[h], vsem.at[h])

    def remote(src, dst, send, recv, to):
        return pltpu.make_async_remote_copy(
            src_ref=src, dst_ref=dst, send_sem=send, recv_sem=recv,
            device_id={"seq": to}, device_id_type=pl.DeviceIdType.MESH,
        )

    def q_near(c, j):
        ref = qall.at[place, quad, :, span(c)]
        return remote(ref, ref, ns.at[c, j], nr.at[c, j], near(j))

    def q_far(c, i):
        ref = qall.at[place, quad, :, span(c)]
        return remote(ref, ref, fs.at[c, i], fr.at[c, i], far(i))

    def q_relay(c, i, j):
        ref = qall.at[place, last_quad(i), :, span(c)]
        return remote(ref, ref, rs.at[c, i, j], rr.at[c, i, j], near(j))

    def x_send(c, j):
        return remote(out.at[next_place(j), :, :, span(c)], xin.at[j, :, :, span(c)],
                      xs.at[c, j], xr.at[c, j], near(j))

    def t_send(j):
        return remote(tout.at[j], tin.at[j], ts.at[j], tr.at[j], near(j))

    def z_send(c, i):
        return remote(zout.at[next_quad(i), :, span(c)], zin.at[i, :, span(c)],
                      zs.at[c, i], zr.at[c, i], far(i))

    def y_send(i):
        return remote(zstat.at[next_quad(i)], ystat.at[i], ys.at[i], yr.at[i], far(i))

    def each_near(step):
        for j in NEAR:
            step(j)

    barrier = pltpu.get_barrier_semaphore()

    def greet(to):
        pl.semaphore_signal(
            barrier, inc=1, device_id={"seq": to}, device_id_type=pl.DeviceIdType.MESH)

    over(1, quads, lambda i: greet(far(i)))
    each_near(lambda j: greet(near(j)))
    own = pltpu.make_async_copy(q_hbm, qall.at[place, quad], own_sem)
    own.start()
    for h in range(heads):
        k_copy(h).start()
        v_copy(h).start()
    stat[...] = jnp.zeros_like(stat)
    zstat[...] = jnp.zeros_like(zstat)
    own.wait()
    pl.semaphore_wait(barrier, quads - 1 + QUAD - 1)

    for c in range(chunks):
        over(1, quads, lambda i: q_far(c, i).start())
    for c in range(chunks):
        each_near(lambda j: q_near(c, j).start())

    def forward(c):
        def step(i):
            q_far(c, i).wait_recv()
            each_near(lambda j: q_relay(c, i, j).start())
        over(1, quads, step)

    for c in range(chunks):
        forward(c)

    group = min(quads, 2)
    count = QUAD * group * rows

    def attend(c, g):
        base = g * group
        scores = [
            lax.dot_general(
                qall[:, pl.ds(base, group), :, cols(h)].reshape(count, HEAD_DIM),
                kbuf[h], (((1,), (1,)), ((), ())), preferred_element_type=jnp.float32,
            )
            for h in heads_of(c)
        ]
        for h, score in zip(heads_of(c), scores):
            peak = jnp.max(score, axis=-1, keepdims=True)
            weights = jnp.exp((score - peak) * factor)
            sums = jnp.sum(weights, axis=-1, keepdims=True)
            context = jnp.dot(
                weights.astype(jnp.bfloat16), vbuf[h], preferred_element_type=jnp.float32
            ) / sums
            shape = (QUAD, group, rows, HEAD_DIM)
            out[:, pl.ds(base, group), :, cols(h)] = encode(context).reshape(shape)
            local[:, pl.ds(base, group), :, cols(h)] = context.reshape(shape)
            stat[:, pl.ds(base, group), :, pl.ds(h, 1)] = (
                peak * factor + jnp.log(sums)
            ).reshape(QUAD, group, rows, 1)

    def send_stat(j):
        tout[j] = stat[next_place(j)].reshape(quads * rows, LANES).T[: tout.shape[1]]
        t_send(j).start()

    for c in range(chunks):
        for h in heads_of(c):
            k_copy(h).wait()
            v_copy(h).wait()
        each_near(lambda j: q_near(c, j).wait_recv())
        over(1, quads, lambda i: each_near(lambda j: q_relay(c, i, j).wait_recv()))
        over(0, quads // group, functools.partial(attend, c))
        if c == chunks - 1:
            each_near(send_stat)
        each_near(lambda j: x_send(c, j).start())

    theirs = []
    for j in range(1, QUAD):
        t_send(j).wait_recv()
        theirs.append(tin[j].T)
    shares = []
    for h in range(heads):
        logs = [stat[place, :, :, pl.ds(h, 1)]]
        logs += [flat[:, h : h + 1].reshape(quads, rows, 1) for flat in theirs]
        top = functools.reduce(jnp.maximum, logs)
        parts = [jnp.exp(log - top) for log in logs]
        total = functools.reduce(jnp.add, parts)
        zstat[:, :, pl.ds(h, 1)] = top + jnp.log(total)
        shares.append([part / total for part in parts])
    over(1, quads, lambda i: y_send(i).start())
    ystat[0] = zstat[quad]
    for c in range(chunks):
        each_near(lambda j: x_send(c, j).wait_recv())
        for h in heads_of(c):
            value = local[place, :, :, cols(h)] * shares[h][0]
            for j in range(1, QUAD):
                value = value + decode(xin[j, :, :, cols(h)]) * shares[h][j]
            zout[:, :, cols(h)] = encode(value)
        over(1, quads, lambda i: z_send(c, i).start())

    over(1, quads, lambda i: y_send(i).wait_recv())
    logs = ystat[...]
    part = jnp.exp(logs - jnp.max(logs, axis=0, keepdims=True))
    ystat[...] = part / jnp.sum(part, axis=0, keepdims=True)
    for c in range(chunks):
        over(1, quads, lambda i: z_send(c, i).wait_recv())
        for h in heads_of(c):
            total = decode(zout[quad, :, cols(h)]) * ystat[0, :, pl.ds(h, 1)]
            for i in range(1, quads):
                total = total + decode(zin[i, :, cols(h)]) * ystat[i, :, pl.ds(h, 1)]
            o_ref[:, cols(h)] = total.astype(o_ref.dtype)

    for c in range(chunks):
        each_near(lambda j: q_near(c, j).wait_send())
        over(1, quads, lambda i: q_far(c, i).wait_send())
        over(1, quads, lambda i: each_near(lambda j: q_relay(c, i, j).wait_send()))
        each_near(lambda j: x_send(c, j).wait_send())
        over(1, quads, lambda i: z_send(c, i).wait_send())
    each_near(lambda j: t_send(j).wait_send())
    over(1, quads, lambda i: y_send(i).wait_send())


def body(n, queries, keys, values):
    rows, columns = queries.shape
    depth = keys.shape[0]
    heads = columns // HEAD_DIM
    chunks = len(split_heads(heads))
    quads = n // QUAD
    high = 8 * pl.cdiv(heads, 8)
    dma = pltpu.SemaphoreType.DMA
    hbm = pl.BlockSpec(memory_space=pltpu.HBM)
    return pl.pallas_call(
        functools.partial(kernel, n),
        out_shape=jax.ShapeDtypeStruct((rows, columns), jnp.bfloat16),
        in_specs=[hbm, hbm, hbm],
        out_specs=pl.BlockSpec(memory_space=pltpu.VMEM),
        scratch_shapes=[
            pltpu.VMEM((QUAD, quads, rows, columns), jnp.bfloat16),
            pltpu.VMEM((heads, depth, HEAD_DIM), jnp.bfloat16),
            pltpu.VMEM((heads, depth, HEAD_DIM), jnp.bfloat16),
            pltpu.VMEM((QUAD, quads, rows, columns), jnp.float32),
            pltpu.VMEM((QUAD, quads, rows, LANES), jnp.float32),
            pltpu.VMEM((QUAD, quads, rows, columns), LINK),
            pltpu.VMEM((QUAD, quads, rows, columns), LINK),
            pltpu.VMEM((quads, rows, columns), LINK),
            pltpu.VMEM((quads, rows, columns), LINK),
            pltpu.VMEM((QUAD, high, quads * rows), jnp.float32),
            pltpu.VMEM((QUAD, high, quads * rows), jnp.float32),
            pltpu.VMEM((quads, rows, LANES), jnp.float32),
            pltpu.VMEM((quads, rows, LANES), jnp.float32),
            dma, dma((heads,)), dma((heads,)),
            dma((chunks, QUAD)), dma((chunks, QUAD)),
            dma((chunks, quads)), dma((chunks, quads)),
            dma((chunks, quads, QUAD)), dma((chunks, quads, QUAD)),
            dma((chunks, QUAD)), dma((chunks, QUAD)),
            dma((QUAD,)), dma((QUAD,)),
            dma((chunks, quads)), dma((chunks, quads)),
            dma((quads,)), dma((quads,)),
        ],
        compiler_params=pltpu.CompilerParams(
            collective_id=0, has_side_effects=True, vmem_limit_bytes=56500000
        ),
        name="attend",
    )(queries, keys, values)


def solution(mesh):
    spec = P(("groups", "seq"), "tensor")
    return jax.shard_map(
        functools.partial(body, mesh.shape["seq"]),
        mesh=mesh,
        in_specs=(spec, spec, spec),
        out_specs=spec,
        check_vma=False,
    )
```

```python
import functools
import math

import jax
import jax.numpy as jnp
from jax import lax
from jax.experimental import pallas as pl
from jax.experimental.pallas import tpu as pltpu
from jax.sharding import PartitionSpec as P

HEAD_DIM = 256
LANES = 128
LINK = jnp.bfloat16
SIZES = (3, 3)
QUAD = 4
NEAR = (1, 3, 2)
FARS = (3, 3)
RAISE = 2.0**60
LOWER = 2.0**-60


def encode(x):
    x = x * RAISE
    return (x * jnp.abs(x)).astype(LINK)


def decode(y):
    y = y.astype(jnp.float32)
    root = jnp.sqrt(jnp.abs(y)) * LOWER
    return jnp.where(y < 0, -root, root)


def over(start, stop, step):
    if stop - start <= 16:
        for index in range(start, stop):
            step(index)
    else:
        lax.fori_loop(start, stop, lambda index, _: (step(index), 0)[1], 0)


def split_heads(heads):
    return SIZES if sum(SIZES) == heads else (heads,)


def kernel(
    n, q_hbm, k_hbm, v_hbm, o_ref, qall, kbuf, vbuf, local, stat, out, xin, zout, zin,
    tout, tin, zstat, ystat, share, mine,
    own_sem, ksem, vsem, ns, nr, fs, fr, rs, rr, xs, xr, os, orr, ts, tr, zs, zr, ys, yr,
):
    rows, columns = q_hbm.shape
    heads = columns // HEAD_DIM
    sizes = split_heads(heads)
    starts = [sum(sizes[:c]) for c in range(len(sizes))]
    chunks = len(sizes)
    far_sizes = FARS if sum(FARS) == heads else (heads,)
    far_starts = [sum(far_sizes[:c]) for c in range(len(far_sizes))]
    factor = 1.0 / math.sqrt(HEAD_DIM)
    quads = n // QUAD
    me = lax.axis_index("seq")
    quad = me // QUAD
    place = lax.rem(me, QUAD)

    def heads_of(c):
        return range(starts[c], starts[c] + sizes[c])

    def cols(h):
        return pl.ds(h * HEAD_DIM, HEAD_DIM)

    def span(c):
        return pl.ds(starts[c] * HEAD_DIM, sizes[c] * HEAD_DIM)

    row, column = place // 2, lax.rem(place, 2)

    def next_place(j):
        return lax.rem(place + j, QUAD)

    def next_quad(i):
        return lax.rem(quad + i, quads)

    def last_quad(i):
        return lax.rem(quad + quads - i, quads)

    def near(j):
        return quad * QUAD + next_place(j)

    def far(i):
        return next_quad(i) * QUAD + place

    def k_copy(h):
        return pltpu.make_async_copy(k_hbm.at[:, cols(h)], kbuf.at[h], ksem.at[h])

    def v_copy(h):
        return pltpu.make_async_copy(v_hbm.at[:, cols(h)], vbuf.at[h], vsem.at[h])

    def remote(src, dst, send, recv, to):
        return pltpu.make_async_remote_copy(
            src_ref=src, dst_ref=dst, send_sem=send, recv_sem=recv,
            device_id={"seq": to}, device_id_type=pl.DeviceIdType.MESH,
        )

    def q_near(j):
        ref = qall.at[place, quad]
        return remote(ref, ref, ns.at[j], nr.at[j], near(j))

    def q_far(c, i):
        ref = qall.at[place, quad, :, pl.ds(far_starts[c] * HEAD_DIM, far_sizes[c] * HEAD_DIM)]
        return remote(ref, ref, fs.at[c, i], fr.at[c, i], far(i))

    def q_relay(c, i, j):
        ref = qall.at[place, last_quad(i), :, span(c)]
        return remote(ref, ref, rs.at[c, i, j], rr.at[c, i, j], near(j))

    def x_send(c, j, i):
        return remote(out.at[next_place(j), next_quad(i), :, span(c)], xin.at[j, i, :, span(c)],
                      xs.at[c, j, i], xr.at[c, j, i], near(j))

    def x_own(j):
        return remote(out.at[next_place(j), quad], xin.at[j, 0], os.at[j], orr.at[j], near(j))

    def t_send(j):
        return remote(tout.at[j], tin.at[j], ts.at[j], tr.at[j], near(j))

    def z_send(c, i):
        return remote(zout.at[i, :, span(c)], zin.at[i, :, span(c)],
                      zs.at[c, i], zr.at[c, i], far(i))

    def y_send(i):
        return remote(zstat.at[next_quad(i)], ystat.at[i], ys.at[i], yr.at[i], far(i))

    def each_near(step):
        for j in NEAR:
            step(j)

    barrier = pltpu.get_barrier_semaphore()

    def greet(to):
        pl.semaphore_signal(
            barrier, inc=1, device_id={"seq": to}, device_id_type=pl.DeviceIdType.MESH)

    over(1, quads, lambda i: greet(far(i)))
    each_near(lambda j: greet(near(j)))
    own = pltpu.make_async_copy(q_hbm, qall.at[place, quad], own_sem)
    own.start()
    for h in range(heads):
        k_copy(h).start()
    stat[...] = jnp.zeros_like(stat)
    zstat[...] = jnp.zeros_like(zstat)
    own.wait()
    pl.semaphore_wait(barrier, quads - 1 + QUAD - 1)

    for c in range(len(far_sizes)):
        over(1, quads, lambda i: q_far(c, i).start())
    each_near(lambda j: q_near(j).start())

    def forward(c):
        def step(i):
            for f in range(len(far_sizes)):
                if starts[c] <= far_starts[f] < starts[c] + sizes[c]:
                    q_far(f, i).wait_recv()
            each_near(lambda j: q_relay(c, i, j).start())
        over(1, quads, step)

    for c in range(chunks):
        forward(c)
    for h in range(heads):
        v_copy(h).start()

    group = min(quads, 2)
    count = QUAD * group * rows

    def attend(c, g):
        base = g * group
        scores = [
            lax.dot_general(
                qall[:, pl.ds(base, group), :, cols(h)].reshape(count, HEAD_DIM),
                kbuf[h], (((1,), (1,)), ((), ())), preferred_element_type=jnp.float32,
            )
            for h in heads_of(c)
        ]
        for h, score in zip(heads_of(c), scores):
            peak = jnp.max(score, axis=-1, keepdims=True)
            weights = jnp.exp((score - peak) * factor)
            sums = jnp.sum(weights, axis=-1, keepdims=True)
            context = jnp.dot(
                weights.astype(jnp.bfloat16), vbuf[h], preferred_element_type=jnp.float32
            ) / sums
            shape = (QUAD, group, rows, HEAD_DIM)
            out[:, pl.ds(base, group), :, cols(h)] = encode(context).reshape(shape)
            local[:, pl.ds(base, group), :, cols(h)] = context.reshape(shape)
            stat[:, pl.ds(base, group), :, pl.ds(h, 1)] = (
                peak * factor + jnp.log(sums)
            ).reshape(QUAD, group, rows, 1)

    def send_stat(j):
        tout[j] = stat[next_place(j)].reshape(quads * rows, LANES).T[: tout.shape[1]]
        t_send(j).start()

    for c in range(chunks):
        for h in heads_of(c):
            k_copy(h).wait()
            v_copy(h).wait()
        if c == 0:
            each_near(lambda j: q_near(j).wait_recv())
        over(1, quads, lambda i: each_near(lambda j: q_relay(c, i, j).wait_recv()))
        over(0, quads // group, functools.partial(attend, c))
        if c == chunks - 1:
            each_near(send_stat)
        over(1, quads, lambda i: each_near(lambda j: x_send(c, j, i).start()))
    each_near(lambda j: x_own(j).start())

    theirs = []
    for j in range(1, QUAD):
        t_send(j).wait_recv()
        theirs.append(tin[j].T)
    shares = []
    for h in range(heads):
        logs = [stat[place, :, :, pl.ds(h, 1)]]
        logs += [flat[:, h : h + 1].reshape(quads, rows, 1) for flat in theirs]
        top = functools.reduce(jnp.maximum, logs)
        parts = [jnp.exp(log - top) for log in logs]
        total = functools.reduce(jnp.add, parts)
        zstat[:, :, pl.ds(h, 1)] = top + jnp.log(total)
        for j in range(QUAD):
            share[j, :, :, pl.ds(h, 1)] = parts[j] / total
    over(1, quads, lambda i: y_send(i).start())
    ystat[0] = zstat[quad]

    def merged(h, i):
        g = next_quad(i)
        value = local[place, g, :, cols(h)] * share[0, g, :, pl.ds(h, 1)]
        for j in range(1, QUAD):
            value = value + decode(xin[j, i, :, cols(h)]) * share[j, g, :, pl.ds(h, 1)]
        return value

    for c in range(chunks):
        def cross(i):
            each_near(lambda j: x_send(c, j, i).wait_recv())
            for h in heads_of(c):
                zout[i, :, cols(h)] = encode(merged(h, i))
            z_send(c, i).start()
        over(1, quads, cross)
    each_near(lambda j: x_own(j).wait_recv())
    for h in range(heads):
        mine[:, cols(h)] = merged(h, 0)

    over(1, quads, lambda i: y_send(i).wait_recv())
    logs = ystat[...]
    part = jnp.exp(logs - jnp.max(logs, axis=0, keepdims=True))
    ystat[...] = part / jnp.sum(part, axis=0, keepdims=True)
    for c in range(chunks):
        over(1, quads, lambda i: z_send(c, i).wait_recv())
        for h in heads_of(c):
            total = mine[:, cols(h)] * ystat[0, :, pl.ds(h, 1)]
            for i in range(1, quads):
                total = total + decode(zin[i, :, cols(h)]) * ystat[i, :, pl.ds(h, 1)]
            o_ref[:, cols(h)] = total.astype(o_ref.dtype)

    for c in range(chunks):
        over(1, quads, lambda i: each_near(lambda j: q_relay(c, i, j).wait_send()))
        over(1, quads, lambda i: each_near(lambda j: x_send(c, j, i).wait_send()))
        over(1, quads, lambda i: z_send(c, i).wait_send())
    for c in range(len(far_sizes)):
        over(1, quads, lambda i: q_far(c, i).wait_send())
    each_near(lambda j: q_near(j).wait_send())
    each_near(lambda j: x_own(j).wait_send())
    each_near(lambda j: t_send(j).wait_send())
    over(1, quads, lambda i: y_send(i).wait_send())


def body(n, queries, keys, values):
    rows, columns = queries.shape
    depth = keys.shape[0]
    heads = columns // HEAD_DIM
    chunks = len(split_heads(heads))
    quads = n // QUAD
    high = 8 * pl.cdiv(heads, 8)
    dma = pltpu.SemaphoreType.DMA
    hbm = pl.BlockSpec(memory_space=pltpu.HBM)
    return pl.pallas_call(
        functools.partial(kernel, n),
        out_shape=jax.ShapeDtypeStruct((rows, columns), jnp.bfloat16),
        in_specs=[hbm, hbm, hbm],
        out_specs=pl.BlockSpec(memory_space=pltpu.VMEM),
        scratch_shapes=[
            pltpu.VMEM((QUAD, quads, rows, columns), jnp.bfloat16),
            pltpu.VMEM((heads, depth, HEAD_DIM), jnp.bfloat16),
            pltpu.VMEM((heads, depth, HEAD_DIM), jnp.bfloat16),
            pltpu.VMEM((QUAD, quads, rows, columns), jnp.float32),
            pltpu.VMEM((QUAD, quads, rows, LANES), jnp.float32),
            pltpu.VMEM((QUAD, quads, rows, columns), LINK),
            pltpu.VMEM((QUAD, quads, rows, columns), LINK),
            pltpu.VMEM((quads, rows, columns), LINK),
            pltpu.VMEM((quads, rows, columns), LINK),
            pltpu.VMEM((QUAD, high, quads * rows), jnp.float32),
            pltpu.VMEM((QUAD, high, quads * rows), jnp.float32),
            pltpu.VMEM((quads, rows, LANES), jnp.float32),
            pltpu.VMEM((quads, rows, LANES), jnp.float32),
            pltpu.VMEM((QUAD, quads, rows, LANES), jnp.float32),
            pltpu.VMEM((rows, columns), jnp.float32),
            dma, dma((heads,)), dma((heads,)),
            dma((QUAD,)), dma((QUAD,)),
            dma((heads, quads)), dma((heads, quads)),
            dma((chunks, quads, QUAD)), dma((chunks, quads, QUAD)),
            dma((chunks, QUAD, quads)), dma((chunks, QUAD, quads)),
            dma((QUAD,)), dma((QUAD,)), dma((QUAD,)), dma((QUAD,)),
            dma((chunks, quads)), dma((chunks, quads)),
            dma((quads,)), dma((quads,)),
        ],
        compiler_params=pltpu.CompilerParams(
            collective_id=0, has_side_effects=True, vmem_limit_bytes=56500000
        ),
        name="attend",
    )(queries, keys, values)


def solution(mesh):
    spec = P(("groups", "seq"), "tensor")
    return jax.shard_map(
        functools.partial(body, mesh.shape["seq"]),
        mesh=mesh,
        in_specs=(spec, spec, spec),
        out_specs=spec,
        check_vma=False,
    )
```

```python
import functools
import math

import jax
import jax.numpy as jnp
from jax import lax
from jax.experimental import pallas as pl
from jax.experimental.pallas import tpu as pltpu
from jax.sharding import PartitionSpec as P

HEAD_DIM = 256
LANES = 128
LINK = jnp.bfloat16
SIZES = (3, 3)
QUAD = 4
NEAR = (1, 3, 2)
FARS = (3, 3)
RAISE = 2.0**60
LOWER = 2.0**-60


def encode(x):
    x = x * RAISE
    return (x * jnp.abs(x)).astype(LINK)


def decode(y):
    y = y.astype(jnp.float32)
    root = jnp.sqrt(jnp.abs(y)) * LOWER
    return jnp.where(y < 0, -root, root)


def over(start, stop, step):
    if stop - start <= 16:
        for index in range(start, stop):
            step(index)
    else:
        lax.fori_loop(start, stop, lambda index, _: (step(index), 0)[1], 0)


def split_heads(heads):
    return SIZES if sum(SIZES) == heads else (heads,)


def kernel(
    n, q_hbm, k_hbm, v_hbm, o_ref, qall, kbuf, vbuf, local, stat, out, xin, zout, zin,
    tout, tin, zstat, ystat, share, mine,
    own_sem, ksem, vsem, ns, nr, fs, fr, rs, rr, xs, xr, os, orr, ts, tr, zs, zr, ys, yr,
):
    rows, columns = q_hbm.shape
    heads = columns // HEAD_DIM
    sizes = split_heads(heads)
    starts = [sum(sizes[:c]) for c in range(len(sizes))]
    chunks = len(sizes)
    far_sizes = FARS if sum(FARS) == heads else (heads,)
    far_starts = [sum(far_sizes[:c]) for c in range(len(far_sizes))]
    factor = 1.0 / math.sqrt(HEAD_DIM)
    quads = n // QUAD
    me = lax.axis_index("seq")
    quad = me // QUAD
    place = lax.rem(me, QUAD)

    def heads_of(c):
        return range(starts[c], starts[c] + sizes[c])

    def cols(h):
        return pl.ds(h * HEAD_DIM, HEAD_DIM)

    def span(c):
        return pl.ds(starts[c] * HEAD_DIM, sizes[c] * HEAD_DIM)

    row, column = place // 2, lax.rem(place, 2)

    def next_place(j):
        return lax.rem(place + j, QUAD)

    def next_quad(i):
        return lax.rem(quad + i, quads)

    def last_quad(i):
        return lax.rem(quad + quads - i, quads)

    def near(j):
        return quad * QUAD + next_place(j)

    def far(i):
        return next_quad(i) * QUAD + place

    def k_copy(h):
        return pltpu.make_async_copy(k_hbm.at[:, cols(h)], kbuf.at[h], ksem.at[h])

    def v_copy(h):
        return pltpu.make_async_copy(v_hbm.at[:, cols(h)], vbuf.at[h], vsem.at[h])

    def remote(src, dst, send, recv, to):
        return pltpu.make_async_remote_copy(
            src_ref=src, dst_ref=dst, send_sem=send, recv_sem=recv,
            device_id={"seq": to}, device_id_type=pl.DeviceIdType.MESH,
        )

    def q_near(j):
        ref = qall.at[place, quad]
        return remote(ref, ref, ns.at[j], nr.at[j], near(j))

    def q_far(c, i):
        ref = qall.at[place, quad, :, pl.ds(far_starts[c] * HEAD_DIM, far_sizes[c] * HEAD_DIM)]
        return remote(ref, ref, fs.at[c, i], fr.at[c, i], far(i))

    def q_relay(c, i, j):
        ref = qall.at[place, last_quad(i), :, span(c)]
        return remote(ref, ref, rs.at[c, i, j], rr.at[c, i, j], near(j))

    def x_send(c, j, i):
        return remote(out.at[next_place(j), next_quad(i), :, span(c)], xin.at[j, i, :, span(c)],
                      xs.at[c, j, i], xr.at[c, j, i], near(j))

    def x_own(j):
        return remote(out.at[next_place(j), quad], xin.at[j, 0], os.at[j], orr.at[j], near(j))

    def t_send(j):
        return remote(tout.at[j], tin.at[j], ts.at[j], tr.at[j], near(j))

    def z_send(c, i):
        return remote(zout.at[i, :, span(c)], zin.at[i, :, span(c)],
                      zs.at[c, i], zr.at[c, i], far(i))

    def y_send(i):
        return remote(zstat.at[next_quad(i)], ystat.at[i], ys.at[i], yr.at[i], far(i))

    def each_near(step):
        for j in NEAR:
            step(j)

    barrier = pltpu.get_barrier_semaphore()

    def greet(to):
        pl.semaphore_signal(
            barrier, inc=1, device_id={"seq": to}, device_id_type=pl.DeviceIdType.MESH)

    over(1, quads, lambda i: greet(far(i)))
    each_near(lambda j: greet(near(j)))
    own = pltpu.make_async_copy(q_hbm, qall.at[place, quad], own_sem)
    own.start()
    for h in range(heads):
        k_copy(h).start()
    stat[...] = jnp.zeros_like(stat)
    zstat[...] = jnp.zeros_like(zstat)
    own.wait()
    pl.semaphore_wait(barrier, quads - 1 + QUAD - 1)

    for c in range(len(far_sizes)):
        over(1, quads, lambda i: q_far(c, i).start())
    each_near(lambda j: q_near(j).start())

    def forward(c):
        def step(i):
            for f in range(len(far_sizes)):
                if starts[c] <= far_starts[f] < starts[c] + sizes[c]:
                    q_far(f, i).wait_recv()
            each_near(lambda j: q_relay(c, i, j).start())
        over(1, quads, step)

    for c in range(chunks):
        forward(c)
    for h in range(heads):
        v_copy(h).start(priority=1)

    group = min(quads, 2)
    count = QUAD * group * rows

    def attend(c, g):
        base = g * group
        scores = [
            lax.dot_general(
                qall[:, pl.ds(base, group), :, cols(h)].reshape(count, HEAD_DIM),
                kbuf[h], (((1,), (1,)), ((), ())), preferred_element_type=jnp.float32,
            )
            for h in heads_of(c)
        ]
        for h, score in zip(heads_of(c), scores):
            peak = jnp.max(score, axis=-1, keepdims=True)
            weights = jnp.exp((score - peak) * factor)
            sums = jnp.sum(weights, axis=-1, keepdims=True)
            context = jnp.dot(
                weights.astype(jnp.bfloat16), vbuf[h], preferred_element_type=jnp.float32
            ) / sums
            shape = (QUAD, group, rows, HEAD_DIM)
            out[:, pl.ds(base, group), :, cols(h)] = encode(context).reshape(shape)
            local[:, pl.ds(base, group), :, cols(h)] = context.reshape(shape)
            stat[:, pl.ds(base, group), :, pl.ds(h, 1)] = (
                peak * factor + jnp.log(sums)
            ).reshape(QUAD, group, rows, 1)

    def send_stat(j):
        tout[j] = stat[next_place(j)].reshape(quads * rows, LANES).T[: tout.shape[1]]
        t_send(j).start()

    for c in range(chunks):
        for h in heads_of(c):
            k_copy(h).wait()
            v_copy(h).wait()
        if c == 0:
            each_near(lambda j: q_near(j).wait_recv())
        over(1, quads, lambda i: each_near(lambda j: q_relay(c, i, j).wait_recv()))
        over(0, quads // group, functools.partial(attend, c))
        if c == chunks - 1:
            each_near(send_stat)
        over(1, quads, lambda i: each_near(lambda j: x_send(c, j, i).start()))
    each_near(lambda j: x_own(j).start())

    each_near(lambda j: q_near(j).wait_send())
    for c in range(len(far_sizes)):
        over(1, quads, lambda i: q_far(c, i).wait_send())
    for c in range(chunks):
        over(1, quads, lambda i: each_near(lambda j: q_relay(c, i, j).wait_send()))

    high = tout.shape[1]
    logs = [stat[place, :, :, pl.ds(0, high)]]
    for j in range(1, QUAD):
        t_send(j).wait_recv()
        logs.append(tin[j].T.reshape(quads, rows, high))
    top = functools.reduce(jnp.maximum, logs)
    parts = [jnp.exp(log - top) for log in logs]
    total = functools.reduce(jnp.add, parts)
    zstat[:, :, pl.ds(0, high)] = top + jnp.log(total)
    for j in range(QUAD):
        share[j, :, :, pl.ds(0, high)] = parts[j] / total
    over(1, quads, lambda i: y_send(i).start())
    ystat[0] = zstat[quad]

    def merged(h, i):
        g = next_quad(i)
        value = local[place, g, :, cols(h)] * share[0, g, :, pl.ds(h, 1)]
        for j in range(1, QUAD):
            value = value + decode(xin[j, i, :, cols(h)]) * share[j, g, :, pl.ds(h, 1)]
        return value

    for c in range(chunks):
        def cross(i):
            each_near(lambda j: x_send(c, j, i).wait_recv())
            for h in heads_of(c):
                zout[i, :, cols(h)] = encode(merged(h, i))
            z_send(c, i).start()
        over(1, quads, cross)
    each_near(lambda j: x_own(j).wait_recv())
    for h in range(heads):
        mine[:, cols(h)] = merged(h, 0)

    for c in range(chunks):
        over(1, quads, lambda i: each_near(lambda j: x_send(c, j, i).wait_send()))
    each_near(lambda j: x_own(j).wait_send())
    each_near(lambda j: t_send(j).wait_send())
    for c in range(chunks):
        over(1, quads, lambda i: z_send(c, i).wait_send())
    over(1, quads, lambda i: y_send(i).wait_send())
    over(1, quads, lambda i: y_send(i).wait_recv())
    logs = ystat[...]
    part = jnp.exp(logs - jnp.max(logs, axis=0, keepdims=True))
    ystat[...] = part / jnp.sum(part, axis=0, keepdims=True)
    for c in range(chunks):
        over(1, quads, lambda i: z_send(c, i).wait_recv())
        for h in heads_of(c):
            total = mine[:, cols(h)] * ystat[0, :, pl.ds(h, 1)]
            for i in range(1, quads):
                total = total + decode(zin[i, :, cols(h)]) * ystat[i, :, pl.ds(h, 1)]
            o_ref[:, cols(h)] = total.astype(o_ref.dtype)


def body(n, queries, keys, values):
    rows, columns = queries.shape
    depth = keys.shape[0]
    heads = columns // HEAD_DIM
    chunks = len(split_heads(heads))
    quads = n // QUAD
    high = 8 * pl.cdiv(heads, 8)
    dma = pltpu.SemaphoreType.DMA
    hbm = pl.BlockSpec(memory_space=pltpu.HBM)
    return pl.pallas_call(
        functools.partial(kernel, n),
        out_shape=jax.ShapeDtypeStruct((rows, columns), jnp.bfloat16),
        in_specs=[hbm, hbm, hbm],
        out_specs=pl.BlockSpec(memory_space=pltpu.VMEM),
        scratch_shapes=[
            pltpu.VMEM((QUAD, quads, rows, columns), jnp.bfloat16),
            pltpu.VMEM((heads, depth, HEAD_DIM), jnp.bfloat16),
            pltpu.VMEM((heads, depth, HEAD_DIM), jnp.bfloat16),
            pltpu.VMEM((QUAD, quads, rows, columns), jnp.float32),
            pltpu.VMEM((QUAD, quads, rows, LANES), jnp.float32),
            pltpu.VMEM((QUAD, quads, rows, columns), LINK),
            pltpu.VMEM((QUAD, quads, rows, columns), LINK),
            pltpu.VMEM((quads, rows, columns), LINK),
            pltpu.VMEM((quads, rows, columns), LINK),
            pltpu.VMEM((QUAD, high, quads * rows), jnp.float32),
            pltpu.VMEM((QUAD, high, quads * rows), jnp.float32),
            pltpu.VMEM((quads, rows, LANES), jnp.float32),
            pltpu.VMEM((quads, rows, LANES), jnp.float32),
            pltpu.VMEM((QUAD, quads, rows, LANES), jnp.float32),
            pltpu.VMEM((rows, columns), jnp.float32),
            dma, dma((heads,)), dma((heads,)),
            dma((QUAD,)), dma((QUAD,)),
            dma((heads, quads)), dma((heads, quads)),
            dma((chunks, quads, QUAD)), dma((chunks, quads, QUAD)),
            dma((chunks, QUAD, quads)), dma((chunks, QUAD, quads)),
            dma((QUAD,)), dma((QUAD,)), dma((QUAD,)), dma((QUAD,)),
            dma((chunks, quads)), dma((chunks, quads)),
            dma((quads,)), dma((quads,)),
        ],
        compiler_params=pltpu.CompilerParams(
            collective_id=0, has_side_effects=True, vmem_limit_bytes=56500000
        ),
        name="attend",
    )(queries, keys, values)


def solution(mesh):
    spec = P(("groups", "seq"), "tensor")
    return jax.shard_map(
        functools.partial(body, mesh.shape["seq"]),
        mesh=mesh,
        in_specs=(spec, spec, spec),
        out_specs=spec,
        check_vma=False,
    )
```

```python
import functools
import math

import jax
import jax.numpy as jnp
from jax import lax
from jax.experimental import pallas as pl
from jax.experimental.pallas import tpu as pltpu
from jax.sharding import PartitionSpec as P

HEAD_DIM = 256
LANES = 128
LINK = jnp.bfloat16
SIZES = (3, 3)
QUAD = 4
NEAR = (1, 3, 2)
FARS = (3, 3)
OWN_SIZES = (6,)
RAISE = 2.0**60
LOWER = 2.0**-60


def encode(x):
    x = x * RAISE
    return (x * jnp.abs(x)).astype(LINK)


def decode(y):
    y = y.astype(jnp.float32)
    root = jnp.sqrt(jnp.abs(y)) * LOWER
    return jnp.where(y < 0, -root, root)


def over(start, stop, step):
    if stop - start <= 16:
        for index in range(start, stop):
            step(index)
    else:
        lax.fori_loop(start, stop, lambda index, _: (step(index), 0)[1], 0)


def split_heads(heads):
    return SIZES if sum(SIZES) == heads else (heads,)


def kernel(
    n, q_hbm, k_hbm, v_hbm, o_ref, qall, kbuf, vbuf, local, stat, out, xin, zout, zin,
    tout, tin, zstat, ystat, share, mine, uout, uin,
    own_sem, ksem, vsem, ns, nr, fs, fr, rs, rr, xs, xr, os, orr, ts, tr, us, ur, zs, zr, ys, yr,
):
    rows, columns = q_hbm.shape
    heads = columns // HEAD_DIM
    sizes = split_heads(heads)
    starts = [sum(sizes[:c]) for c in range(len(sizes))]
    chunks = len(sizes)
    far_sizes = FARS if sum(FARS) == heads else (heads,)
    far_starts = [sum(far_sizes[:c]) for c in range(len(far_sizes))]
    factor = 1.0 / math.sqrt(HEAD_DIM)
    quads = n // QUAD
    me = lax.axis_index("seq")
    quad = me // QUAD
    place = lax.rem(me, QUAD)

    def heads_of(c):
        return range(starts[c], starts[c] + sizes[c])

    def cols(h):
        return pl.ds(h * HEAD_DIM, HEAD_DIM)

    def span(c):
        return pl.ds(starts[c] * HEAD_DIM, sizes[c] * HEAD_DIM)

    row, column = place // 2, lax.rem(place, 2)

    def next_place(j):
        return lax.rem(place + j, QUAD)

    def next_quad(i):
        return lax.rem(quad + i, quads)

    def last_quad(i):
        return lax.rem(quad + quads - i, quads)

    def near(j):
        return quad * QUAD + next_place(j)

    def far(i):
        return next_quad(i) * QUAD + place

    def k_copy(h):
        return pltpu.make_async_copy(k_hbm.at[:, cols(h)], kbuf.at[h], ksem.at[h])

    def v_copy(h):
        return pltpu.make_async_copy(v_hbm.at[:, cols(h)], vbuf.at[h], vsem.at[h])

    def remote(src, dst, send, recv, to):
        return pltpu.make_async_remote_copy(
            src_ref=src, dst_ref=dst, send_sem=send, recv_sem=recv,
            device_id={"seq": to}, device_id_type=pl.DeviceIdType.MESH,
        )

    def q_near(j):
        ref = qall.at[place, quad]
        return remote(ref, ref, ns.at[j], nr.at[j], near(j))

    def q_far(c, i):
        ref = qall.at[place, quad, :, pl.ds(far_starts[c] * HEAD_DIM, far_sizes[c] * HEAD_DIM)]
        return remote(ref, ref, fs.at[c, i], fr.at[c, i], far(i))

    def q_relay(c, i, j):
        ref = qall.at[place, last_quad(i), :, span(c)]
        return remote(ref, ref, rs.at[c, i, j], rr.at[c, i, j], near(j))

    def x_send(c, j, i):
        return remote(out.at[next_place(j), next_quad(i), :, span(c)], xin.at[j, i, :, span(c)],
                      xs.at[c, j, i], xr.at[c, j, i], near(j))

    def x_own(j):
        return remote(out.at[next_place(j), quad], xin.at[j, 0], os.at[j], orr.at[j], near(j))

    def t_send(j):
        return remote(tout.at[j], tin.at[j], ts.at[j], tr.at[j], near(j))

    def u_send(j):
        return remote(uout.at[j], uin.at[j], us.at[j], ur.at[j], near(j))

    def z_send(c, i):
        return remote(zout.at[i, :, span(c)], zin.at[i, :, span(c)],
                      zs.at[c, i], zr.at[c, i], far(i))

    def y_send(i):
        return remote(zstat.at[next_quad(i)], ystat.at[i], ys.at[i], yr.at[i], far(i))

    def each_near(step):
        for j in NEAR:
            step(j)

    barrier = pltpu.get_barrier_semaphore()

    def greet(to):
        pl.semaphore_signal(
            barrier, inc=1, device_id={"seq": to}, device_id_type=pl.DeviceIdType.MESH)

    over(1, quads, lambda i: greet(far(i)))
    each_near(lambda j: greet(near(j)))
    own = pltpu.make_async_copy(q_hbm, qall.at[place, quad], own_sem)
    own.start()
    for h in range(heads):
        k_copy(h).start()
    stat[...] = jnp.zeros_like(stat)
    ystat[0] = jnp.zeros_like(ystat[0])
    zstat[...] = jnp.zeros_like(zstat)
    own.wait()
    pl.semaphore_wait(barrier, quads - 1 + QUAD - 1)

    for c in range(len(far_sizes)):
        over(1, quads, lambda i: q_far(c, i).start())

    core = lax.axis_index("tensor")
    pl.when(core == 1)(lambda: each_near(lambda j: q_near(j).start()))
    def forward(c):
        def step(i):
            for f in range(len(far_sizes)):
                if starts[c] <= far_starts[f] < starts[c] + sizes[c]:
                    q_far(f, i).wait_recv()
            each_near(lambda j: q_relay(c, i, j).start())
        over(1, quads, step)

    for c in range(chunks):
        forward(c)
    pl.when(core == 0)(lambda: each_near(lambda j: q_near(j).start()))
    for h in range(heads):
        v_copy(h).start(priority=1)

    def attend(hs, i):
        g = next_quad(i)
        scores = [
            lax.dot_general(
                qall[:, g, :, cols(h)].reshape(QUAD * rows, HEAD_DIM),
                kbuf[h], (((1,), (1,)), ((), ())), preferred_element_type=jnp.float32,
            )
            for h in hs
        ]
        for h, score in zip(hs, scores):
            peak = jnp.max(score, axis=-1, keepdims=True)
            weights = jnp.exp((score - peak) * factor)
            sums = jnp.sum(weights, axis=-1, keepdims=True)
            context = jnp.dot(
                weights.astype(jnp.bfloat16), vbuf[h], preferred_element_type=jnp.float32
            ) / sums
            shape = (QUAD, rows, HEAD_DIM)
            out[:, g, :, cols(h)] = encode(context).reshape(shape)
            local[:, g, :, cols(h)] = context.reshape(shape)
            stat[:, g, :, pl.ds(h, 1)] = (peak * factor + jnp.log(sums)).reshape(QUAD, rows, 1)

    def send_stat(j):
        tout[j] = stat[next_place(j)].reshape(quads * rows, LANES).T[: tout.shape[1]]
        t_send(j).start()

    def send_own_stat(j):
        uout[j] = stat[next_place(j), quad].T[: uout.shape[1]]
        u_send(j).start()

    for c in range(chunks):
        over(1, quads, lambda i: each_near(lambda j: q_relay(c, i, j).wait_recv()))
        for h in heads_of(c):
            k_copy(h).wait()
            v_copy(h).wait()
        over(1, quads, functools.partial(attend, heads_of(c)))
        if c == chunks - 1:
            each_near(send_stat)
        over(1, quads, lambda i: each_near(lambda j: x_send(c, j, i).start()))
    each_near(lambda j: q_near(j).wait_recv())
    parts = OWN_SIZES if sum(OWN_SIZES) == heads else (heads,)
    for p in range(len(parts)):
        attend(range(sum(parts[:p]), sum(parts[: p + 1])), 0)
    each_near(send_own_stat)
    each_near(lambda j: x_own(j).start())

    def weigh(logs):
        top = functools.reduce(jnp.maximum, logs)
        parts = [jnp.exp(log - top) for log in logs]
        total = functools.reduce(jnp.add, parts)
        return top + jnp.log(total), [part / total for part in parts]

    each_near(lambda j: t_send(j).wait_recv())
    flats = [tin[j].T for j in range(1, QUAD)]
    for h in range(heads):
        logs = [stat[place, :, :, pl.ds(h, 1)]]
        logs += [flat[:, h : h + 1].reshape(quads, rows, 1) for flat in flats]
        zstat[:, :, pl.ds(h, 1)], shares = weigh(logs)
        for j in range(QUAD):
            share[j, :, :, pl.ds(h, 1)] = shares[j]
    over(1, quads, lambda i: y_send(i).start())

    def merged(h, i):
        g = next_quad(i)
        value = local[place, g, :, cols(h)] * share[0, g, :, pl.ds(h, 1)]
        for j in range(1, QUAD):
            value = value + decode(xin[j, i, :, cols(h)]) * share[j, g, :, pl.ds(h, 1)]
        return value

    for c in range(chunks):
        def cross(i):
            each_near(lambda j: x_send(c, j, i).wait_recv())
            for h in heads_of(c):
                zout[i, :, cols(h)] = encode(merged(h, i))
            z_send(c, i).start()
        over(1, quads, cross)
    each_near(lambda j: u_send(j).wait_recv())
    flats = [uin[j].T for j in range(1, QUAD)]
    for h in range(heads):
        logs = [stat[place, quad, :, pl.ds(h, 1)]] + [flat[:, h : h + 1] for flat in flats]
        ystat[0, :, pl.ds(h, 1)], shares = weigh(logs)
        for j in range(QUAD):
            share[j, quad, :, pl.ds(h, 1)] = shares[j]
    each_near(lambda j: x_own(j).wait_recv())
    for h in range(heads):
        mine[:, cols(h)] = merged(h, 0)

    over(1, quads, lambda i: y_send(i).wait_recv())
    logs = ystat[...]
    part = jnp.exp(logs - jnp.max(logs, axis=0, keepdims=True))
    ystat[...] = part / jnp.sum(part, axis=0, keepdims=True)
    for c in range(chunks):
        over(1, quads, lambda i: z_send(c, i).wait_recv())
        for h in heads_of(c):
            total = mine[:, cols(h)] * ystat[0, :, pl.ds(h, 1)]
            for i in range(1, quads):
                total = total + decode(zin[i, :, cols(h)]) * ystat[i, :, pl.ds(h, 1)]
            o_ref[:, cols(h)] = total.astype(o_ref.dtype)

    for c in range(chunks):
        over(1, quads, lambda i: each_near(lambda j: q_relay(c, i, j).wait_send()))
        over(1, quads, lambda i: each_near(lambda j: x_send(c, j, i).wait_send()))
        over(1, quads, lambda i: z_send(c, i).wait_send())
    for c in range(len(far_sizes)):
        over(1, quads, lambda i: q_far(c, i).wait_send())
    each_near(lambda j: q_near(j).wait_send())
    each_near(lambda j: x_own(j).wait_send())
    each_near(lambda j: t_send(j).wait_send())
    each_near(lambda j: u_send(j).wait_send())
    over(1, quads, lambda i: y_send(i).wait_send())


def body(n, queries, keys, values):
    rows, columns = queries.shape
    depth = keys.shape[0]
    heads = columns // HEAD_DIM
    chunks = len(split_heads(heads))
    quads = n // QUAD
    high = 8 * pl.cdiv(heads, 8)
    dma = pltpu.SemaphoreType.DMA
    hbm = pl.BlockSpec(memory_space=pltpu.HBM)
    return pl.pallas_call(
        functools.partial(kernel, n),
        out_shape=jax.ShapeDtypeStruct((rows, columns), jnp.bfloat16),
        in_specs=[hbm, hbm, hbm],
        out_specs=pl.BlockSpec(memory_space=pltpu.VMEM),
        scratch_shapes=[
            pltpu.VMEM((QUAD, quads, rows, columns), jnp.bfloat16),
            pltpu.VMEM((heads, depth, HEAD_DIM), jnp.bfloat16),
            pltpu.VMEM((heads, depth, HEAD_DIM), jnp.bfloat16),
            pltpu.VMEM((QUAD, quads, rows, columns), jnp.float32),
            pltpu.VMEM((QUAD, quads, rows, LANES), jnp.float32),
            pltpu.VMEM((QUAD, quads, rows, columns), LINK),
            pltpu.VMEM((QUAD, quads, rows, columns), LINK),
            pltpu.VMEM((quads, rows, columns), LINK),
            pltpu.VMEM((quads, rows, columns), LINK),
            pltpu.VMEM((QUAD, high, quads * rows), jnp.float32),
            pltpu.VMEM((QUAD, high, quads * rows), jnp.float32),
            pltpu.VMEM((quads, rows, LANES), jnp.float32),
            pltpu.VMEM((quads, rows, LANES), jnp.float32),
            pltpu.VMEM((QUAD, quads, rows, LANES), jnp.float32),
            pltpu.VMEM((rows, columns), jnp.float32),
            pltpu.VMEM((QUAD, high, rows), jnp.float32),
            pltpu.VMEM((QUAD, high, rows), jnp.float32),
            dma, dma((heads,)), dma((heads,)),
            dma((QUAD,)), dma((QUAD,)),
            dma((heads, quads)), dma((heads, quads)),
            dma((chunks, quads, QUAD)), dma((chunks, quads, QUAD)),
            dma((chunks, QUAD, quads)), dma((chunks, QUAD, quads)),
            dma((QUAD,)), dma((QUAD,)), dma((QUAD,)), dma((QUAD,)), dma((QUAD,)), dma((QUAD,)),
            dma((chunks, quads)), dma((chunks, quads)),
            dma((quads,)), dma((quads,)),
        ],
        compiler_params=pltpu.CompilerParams(
            collective_id=0, has_side_effects=True, vmem_limit_bytes=56500000
        ),
        name="attend",
    )(queries, keys, values)


def solution(mesh):
    spec = P(("groups", "seq"), "tensor")
    return jax.shard_map(
        functools.partial(body, mesh.shape["seq"]),
        mesh=mesh,
        in_specs=(spec, spec, spec),
        out_specs=spec,
        check_vma=False,
    )
```

```python
import functools
import math

import jax
import jax.numpy as jnp
from jax import lax
from jax.experimental import pallas as pl
from jax.experimental.pallas import tpu as pltpu
from jax.sharding import PartitionSpec as P

HEAD_DIM = 256
LANES = 128
LINK = jnp.bfloat16
SIZES = (3, 3)
QUAD = 4
NEAR = (1, 3, 2)
FARS = (3, 3)
RAISE = 2.0**60
LOWER = 2.0**-60


def encode(x):
    x = x * RAISE
    return (x * jnp.abs(x)).astype(LINK)


def decode(y):
    y = y.astype(jnp.float32)
    root = jnp.sqrt(jnp.abs(y)) * LOWER
    return jnp.where(y < 0, -root, root)


def over(start, stop, step):
    if stop - start <= 16:
        for index in range(start, stop):
            step(index)
    else:
        lax.fori_loop(start, stop, lambda index, _: (step(index), 0)[1], 0)


def split_heads(heads):
    return SIZES if sum(SIZES) == heads else (heads,)


def kernel(
    n, q_hbm, k_hbm, v_hbm, o_ref, qall, kbuf, vbuf, local, stat, out, xin, zout, zin,
    tout, tin, zstat, ystat, share, mine,
    own_sem, ksem, vsem, ns, nr, fs, fr, rs, rr, xs, xr, os, orr, ts, tr, zs, zr, ys, yr,
):
    rows, columns = q_hbm.shape
    heads = columns // HEAD_DIM
    sizes = split_heads(heads)
    starts = [sum(sizes[:c]) for c in range(len(sizes))]
    chunks = len(sizes)
    far_sizes = FARS if sum(FARS) == heads else (heads,)
    far_starts = [sum(far_sizes[:c]) for c in range(len(far_sizes))]
    factor = 1.0 / math.sqrt(HEAD_DIM)
    quads = n // QUAD
    me = lax.axis_index("seq")
    quad = me // QUAD
    place = lax.rem(me, QUAD)

    def heads_of(c):
        return range(starts[c], starts[c] + sizes[c])

    def cols(h):
        return pl.ds(h * HEAD_DIM, HEAD_DIM)

    def span(c):
        return pl.ds(starts[c] * HEAD_DIM, sizes[c] * HEAD_DIM)

    row, column = place // 2, lax.rem(place, 2)

    def next_place(j):
        return lax.rem(place + j, QUAD)

    def next_quad(i):
        return lax.rem(quad + i, quads)

    def last_quad(i):
        return lax.rem(quad + quads - i, quads)

    def near(j):
        return quad * QUAD + next_place(j)

    def far(i):
        return next_quad(i) * QUAD + place

    def k_copy(h):
        return pltpu.make_async_copy(k_hbm.at[:, cols(h)], kbuf.at[h], ksem.at[h])

    def v_copy(h):
        return pltpu.make_async_copy(v_hbm.at[:, cols(h)], vbuf.at[h], vsem.at[h])

    def remote(src, dst, send, recv, to):
        return pltpu.make_async_remote_copy(
            src_ref=src, dst_ref=dst, send_sem=send, recv_sem=recv,
            device_id={"seq": to}, device_id_type=pl.DeviceIdType.MESH,
        )

    def q_near(j):
        ref = qall.at[place, quad]
        return remote(ref, ref, ns.at[j], nr.at[j], near(j))

    def q_far(c, i):
        ref = qall.at[place, quad, :, pl.ds(far_starts[c] * HEAD_DIM, far_sizes[c] * HEAD_DIM)]
        return remote(ref, ref, fs.at[c, i], fr.at[c, i], far(i))

    def q_relay(c, i, j):
        ref = qall.at[place, last_quad(i), :, span(c)]
        return remote(ref, ref, rs.at[c, i, j], rr.at[c, i, j], near(j))

    def x_send(c, j, i):
        return remote(out.at[next_place(j), next_quad(i), :, span(c)], xin.at[j, i, :, span(c)],
                      xs.at[c, j, i], xr.at[c, j, i], near(j))

    def x_own(j):
        return remote(out.at[next_place(j), quad], xin.at[j, 0], os.at[j], orr.at[j], near(j))

    def t_send(j):
        return remote(tout.at[j], tin.at[j], ts.at[j], tr.at[j], near(j))

    def z_send(c, i):
        return remote(zout.at[i, :, span(c)], zin.at[i, :, span(c)],
                      zs.at[c, i], zr.at[c, i], far(i))

    def y_send(i):
        return remote(zstat.at[next_quad(i)], ystat.at[i], ys.at[i], yr.at[i], far(i))

    def each_near(step):
        for j in NEAR:
            step(j)

    barrier = pltpu.get_barrier_semaphore()

    def greet(to):
        pl.semaphore_signal(
            barrier, inc=1, device_id={"seq": to}, device_id_type=pl.DeviceIdType.MESH)

    over(1, quads, lambda i: greet(far(i)))
    each_near(lambda j: greet(near(j)))
    own = pltpu.make_async_copy(q_hbm, qall.at[place, quad], own_sem)
    own.start()
    for h in range(heads):
        k_copy(h).start()
    stat[...] = jnp.zeros_like(stat)
    zstat[...] = jnp.zeros_like(zstat)
    own.wait()
    pl.semaphore_wait(barrier, quads - 1 + QUAD - 1)

    for c in range(len(far_sizes)):
        over(1, quads, lambda i: q_far(c, i).start())
    each_near(lambda j: q_near(j).start())

    def forward(c):
        def step(i):
            for f in range(len(far_sizes)):
                if starts[c] <= far_starts[f] < starts[c] + sizes[c]:
                    q_far(f, i).wait_recv()
            each_near(lambda j: q_relay(c, i, j).start())
        over(1, quads, step)

    for c in range(chunks):
        forward(c)
    for h in range(heads):
        v_copy(h).start(priority=1)

    group = min(quads, 2)
    count = QUAD * group * rows

    def attend(c, g):
        base = g * group
        scores = [
            lax.dot_general(
                qall[:, pl.ds(base, group), :, cols(h)].reshape(count, HEAD_DIM),
                kbuf[h], (((1,), (1,)), ((), ())), preferred_element_type=jnp.float32,
            )
            for h in heads_of(c)
        ]
        for h, score in zip(heads_of(c), scores):
            peak = jnp.max(score, axis=-1, keepdims=True)
            weights = jnp.exp((score - peak) * factor)
            sums = jnp.sum(weights, axis=-1, keepdims=True)
            context = jnp.dot(
                weights.astype(jnp.bfloat16), vbuf[h], preferred_element_type=jnp.float32
            ) / sums
            shape = (QUAD, group, rows, HEAD_DIM)
            out[:, pl.ds(base, group), :, cols(h)] = encode(context).reshape(shape)
            local[:, pl.ds(base, group), :, cols(h)] = context.reshape(shape)
            stat[:, pl.ds(base, group), :, pl.ds(h, 1)] = (
                peak * factor + jnp.log(sums)
            ).reshape(QUAD, group, rows, 1)

    def send_stat(j):
        tout[j] = stat[next_place(j)].reshape(quads * rows, LANES).T[: tout.shape[1]]
        t_send(j).start()

    for c in range(chunks):
        for h in heads_of(c):
            k_copy(h).wait()
            v_copy(h).wait()
        if c == 0:
            each_near(lambda j: q_near(j).wait_recv())
        over(1, quads, lambda i: each_near(lambda j: q_relay(c, i, j).wait_recv()))
        over(0, quads // group, functools.partial(attend, c))
        if c == chunks - 1:
            each_near(send_stat)
        over(1, quads, lambda i: each_near(lambda j: x_send(c, j, i).start()))
    each_near(lambda j: q_near(j).wait_send())
    for c in range(len(far_sizes)):
        over(1, quads, lambda i: q_far(c, i).wait_send())
    for c in range(chunks):
        over(1, quads, lambda i: each_near(lambda j: q_relay(c, i, j).wait_send()))

    each_near(lambda j: x_own(j).start())
    high = tout.shape[1]
    logs = [stat[place, :, :, pl.ds(0, high)]]
    for j in range(1, QUAD):
        t_send(j).wait_recv()
        logs.append(tin[j].T.reshape(quads, rows, high))
    top = functools.reduce(jnp.maximum, logs)
    parts = [jnp.exp(log - top) for log in logs]
    total = functools.reduce(jnp.add, parts)
    zstat[:, :, pl.ds(0, high)] = top + jnp.log(total)
    for j in range(QUAD):
        share[j, :, :, pl.ds(0, high)] = parts[j] / total
    over(1, quads, lambda i: y_send(i).start())
    ystat[0] = zstat[quad]

    def merged(h, i):
        g = next_quad(i)
        value = local[place, g, :, cols(h)] * share[0, g, :, pl.ds(h, 1)]
        for j in range(1, QUAD):
            value = value + decode(xin[j, i, :, cols(h)]) * share[j, g, :, pl.ds(h, 1)]
        return value

    for c in range(chunks):
        def cross(i):
            each_near(lambda j: x_send(c, j, i).wait_recv())
            for h in heads_of(c):
                zout[i, :, cols(h)] = encode(merged(h, i))
            z_send(c, i).start()
        over(1, quads, cross)
    each_near(lambda j: x_own(j).wait_recv())
    for h in range(heads):
        mine[:, cols(h)] = merged(h, 0)

    for c in range(chunks):
        over(1, quads, lambda i: each_near(lambda j: x_send(c, j, i).wait_send()))
    each_near(lambda j: x_own(j).wait_send())
    each_near(lambda j: t_send(j).wait_send())
    for c in range(chunks):
        over(1, quads, lambda i: z_send(c, i).wait_send())
    over(1, quads, lambda i: y_send(i).wait_send())
    over(1, quads, lambda i: y_send(i).wait_recv())
    logs = ystat[...]
    part = jnp.exp(logs - jnp.max(logs, axis=0, keepdims=True))
    ystat[...] = part / jnp.sum(part, axis=0, keepdims=True)
    for c in range(chunks):
        over(1, quads, lambda i: z_send(c, i).wait_recv())
        for h in heads_of(c):
            total = mine[:, cols(h)] * ystat[0, :, pl.ds(h, 1)]
            for i in range(1, quads):
                total = total + decode(zin[i, :, cols(h)]) * ystat[i, :, pl.ds(h, 1)]
            o_ref[:, cols(h)] = total.astype(o_ref.dtype)


def body(n, queries, keys, values):
    rows, columns = queries.shape
    depth = keys.shape[0]
    heads = columns // HEAD_DIM
    chunks = len(split_heads(heads))
    quads = n // QUAD
    high = 8 * pl.cdiv(heads, 8)
    dma = pltpu.SemaphoreType.DMA
    hbm = pl.BlockSpec(memory_space=pltpu.HBM)
    return pl.pallas_call(
        functools.partial(kernel, n),
        out_shape=jax.ShapeDtypeStruct((rows, columns), jnp.bfloat16),
        in_specs=[hbm, hbm, hbm],
        out_specs=pl.BlockSpec(memory_space=pltpu.VMEM),
        scratch_shapes=[
            pltpu.VMEM((QUAD, quads, rows, columns), jnp.bfloat16),
            pltpu.VMEM((heads, depth, HEAD_DIM), jnp.bfloat16),
            pltpu.VMEM((heads, depth, HEAD_DIM), jnp.bfloat16),
            pltpu.VMEM((QUAD, quads, rows, columns), jnp.float32),
            pltpu.VMEM((QUAD, quads, rows, LANES), jnp.float32),
            pltpu.VMEM((QUAD, quads, rows, columns), LINK),
            pltpu.VMEM((QUAD, quads, rows, columns), LINK),
            pltpu.VMEM((quads, rows, columns), LINK),
            pltpu.VMEM((quads, rows, columns), LINK),
            pltpu.VMEM((QUAD, high, quads * rows), jnp.float32),
            pltpu.VMEM((QUAD, high, quads * rows), jnp.float32),
            pltpu.VMEM((quads, rows, LANES), jnp.float32),
            pltpu.VMEM((quads, rows, LANES), jnp.float32),
            pltpu.VMEM((QUAD, quads, rows, LANES), jnp.float32),
            pltpu.VMEM((rows, columns), jnp.float32),
            dma, dma((heads,)), dma((heads,)),
            dma((QUAD,)), dma((QUAD,)),
            dma((heads, quads)), dma((heads, quads)),
            dma((chunks, quads, QUAD)), dma((chunks, quads, QUAD)),
            dma((chunks, QUAD, quads)), dma((chunks, QUAD, quads)),
            dma((QUAD,)), dma((QUAD,)), dma((QUAD,)), dma((QUAD,)),
            dma((chunks, quads)), dma((chunks, quads)),
            dma((quads,)), dma((quads,)),
        ],
        compiler_params=pltpu.CompilerParams(
            collective_id=0, has_side_effects=True, vmem_limit_bytes=56500000
        ),
        name="attend",
    )(queries, keys, values)


def solution(mesh):
    spec = P(("groups", "seq"), "tensor")
    return jax.shard_map(
        functools.partial(body, mesh.shape["seq"]),
        mesh=mesh,
        in_specs=(spec, spec, spec),
        out_specs=spec,
        check_vma=False,
    )
```

```python
import functools
import math

import jax
import jax.numpy as jnp
from jax import lax
from jax.experimental import pallas as pl
from jax.experimental.pallas import tpu as pltpu
from jax.sharding import PartitionSpec as P

HEAD_DIM = 256
LANES = 128
LINK = jnp.bfloat16
SIZES = (3, 3)
QUAD = 4
NEAR = (1, 3, 2)
FARS = (3, 3)
RAISE = 2.0**60
LOWER = 2.0**-60


def encode(x):
    x = x * RAISE
    return (x * jnp.abs(x)).astype(LINK)


def decode(y):
    y = y.astype(jnp.float32)
    root = jnp.sqrt(jnp.abs(y)) * LOWER
    return jnp.where(y < 0, -root, root)


def over(start, stop, step):
    if stop - start <= 16:
        for index in range(start, stop):
            step(index)
    else:
        lax.fori_loop(start, stop, lambda index, _: (step(index), 0)[1], 0)


def split_heads(heads):
    return SIZES if sum(SIZES) == heads else (heads,)


def kernel(
    n, q_hbm, k_hbm, v_hbm, o_ref, qall, kbuf, vbuf, local, stat, out, xin, zout, zin,
    tout, tin, zstat, ystat, share, mine,
    own_sem, ksem, vsem, ns, nr, fs, fr, rs, rr, xs, xr, os, orr, ts, tr, zs, zr, ys, yr,
):
    rows, columns = q_hbm.shape
    heads = columns // HEAD_DIM
    sizes = split_heads(heads)
    starts = [sum(sizes[:c]) for c in range(len(sizes))]
    chunks = len(sizes)
    far_sizes = FARS if sum(FARS) == heads else (heads,)
    far_starts = [sum(far_sizes[:c]) for c in range(len(far_sizes))]
    factor = 1.0 / math.sqrt(HEAD_DIM)
    quads = n // QUAD
    me = lax.axis_index("seq")
    quad = me // QUAD
    place = lax.rem(me, QUAD)

    def heads_of(c):
        return range(starts[c], starts[c] + sizes[c])

    def cols(h):
        return pl.ds(h * HEAD_DIM, HEAD_DIM)

    def span(c):
        return pl.ds(starts[c] * HEAD_DIM, sizes[c] * HEAD_DIM)

    row, column = place // 2, lax.rem(place, 2)

    def next_place(j):
        return lax.rem(place + j, QUAD)

    def next_quad(i):
        return lax.rem(quad + i, quads)

    def last_quad(i):
        return lax.rem(quad + quads - i, quads)

    def near(j):
        return quad * QUAD + next_place(j)

    def far(i):
        return next_quad(i) * QUAD + place

    def k_copy(h):
        return pltpu.make_async_copy(k_hbm.at[:, cols(h)], kbuf.at[h], ksem.at[h])

    def v_copy(h):
        return pltpu.make_async_copy(v_hbm.at[:, cols(h)], vbuf.at[h], vsem.at[h])

    def remote(src, dst, send, recv, to):
        return pltpu.make_async_remote_copy(
            src_ref=src, dst_ref=dst, send_sem=send, recv_sem=recv,
            device_id={"seq": to}, device_id_type=pl.DeviceIdType.MESH,
        )

    def q_near(j):
        ref = qall.at[place, quad]
        return remote(ref, ref, ns.at[j], nr.at[j], near(j))

    def q_far(c, i):
        ref = qall.at[place, quad, :, pl.ds(far_starts[c] * HEAD_DIM, far_sizes[c] * HEAD_DIM)]
        return remote(ref, ref, fs.at[c, i], fr.at[c, i], far(i))

    def q_relay(c, i, j):
        ref = qall.at[place, last_quad(i), :, span(c)]
        return remote(ref, ref, rs.at[c, i, j], rr.at[c, i, j], near(j))

    def x_send(c, j, i):
        return remote(out.at[next_place(j), next_quad(i), :, span(c)], xin.at[j, i, :, span(c)],
                      xs.at[c, j, i], xr.at[c, j, i], near(j))

    def x_own(j):
        return remote(out.at[next_place(j), quad], xin.at[j, 0], os.at[j], orr.at[j], near(j))

    def t_send(j):
        return remote(tout.at[j], tin.at[j], ts.at[j], tr.at[j], near(j))

    def z_send(c, i):
        return remote(zout.at[i, :, span(c)], zin.at[i, :, span(c)],
                      zs.at[c, i], zr.at[c, i], far(i))

    def y_send(i):
        return remote(zstat.at[next_quad(i)], ystat.at[i], ys.at[i], yr.at[i], far(i))

    def each_near(step):
        for j in NEAR:
            step(j)

    barrier = pltpu.get_barrier_semaphore()

    def greet(to):
        pl.semaphore_signal(
            barrier, inc=1, device_id={"seq": to}, device_id_type=pl.DeviceIdType.MESH)

    each_near(lambda j: greet(near(j)))
    over(1, quads, lambda i: greet(far(i)))
    own = pltpu.make_async_copy(q_hbm, qall.at[place, quad], own_sem)
    own.start()
    for h in range(heads):
        k_copy(h).start()
    stat[...] = jnp.zeros_like(stat)
    zstat[...] = jnp.zeros_like(zstat)
    own.wait()
    pl.semaphore_wait(barrier, quads - 1 + QUAD - 1)

    for c in range(len(far_sizes)):
        over(1, quads, lambda i: q_far(c, i).start())
    each_near(lambda j: q_near(j).start())

    def forward(c):
        def step(i):
            for f in range(len(far_sizes)):
                if starts[c] <= far_starts[f] < starts[c] + sizes[c]:
                    q_far(f, i).wait_recv()
            each_near(lambda j: q_relay(c, i, j).start())
        over(1, quads, step)

    for c in range(chunks):
        forward(c)
    for h in range(heads):
        v_copy(h).start(priority=1)

    group = min(quads, 2)
    count = QUAD * group * rows

    def attend(c, g):
        base = g * group
        scores = [
            lax.dot_general(
                qall[:, pl.ds(base, group), :, cols(h)].reshape(count, HEAD_DIM),
                kbuf[h], (((1,), (1,)), ((), ())), preferred_element_type=jnp.float32,
            )
            for h in heads_of(c)
        ]
        for h, score in zip(heads_of(c), scores):
            peak = jnp.max(score, axis=-1, keepdims=True)
            weights = jnp.exp((score - peak) * factor)
            sums = jnp.sum(weights, axis=-1, keepdims=True)
            context = jnp.dot(
                weights.astype(jnp.bfloat16), vbuf[h], preferred_element_type=jnp.float32
            ) * (1.0 / sums)
            shape = (QUAD, group, rows, HEAD_DIM)
            out[:, pl.ds(base, group), :, cols(h)] = encode(context).reshape(shape)
            local[:, pl.ds(base, group), :, cols(h)] = context.reshape(shape)
            stat[:, pl.ds(base, group), :, pl.ds(h, 1)] = (
                peak * factor + jnp.log(sums)
            ).reshape(QUAD, group, rows, 1)

    def send_stat(j):
        tout[j] = stat[next_place(j)].reshape(quads * rows, LANES).T[: tout.shape[1]]
        t_send(j).start()

    for c in range(chunks):
        for h in heads_of(c):
            k_copy(h).wait()
            v_copy(h).wait()
        if c == 0:
            each_near(lambda j: q_near(j).wait_recv())
        over(1, quads, lambda i: each_near(lambda j: q_relay(c, i, j).wait_recv()))
        over(0, quads // group, functools.partial(attend, c))
        if c == chunks - 1:
            each_near(send_stat)
        over(1, quads, lambda i: each_near(lambda j: x_send(c, j, i).start()))
    each_near(lambda j: x_own(j).start())

    each_near(lambda j: q_near(j).wait_send())
    for c in range(len(far_sizes)):
        over(1, quads, lambda i: q_far(c, i).wait_send())
    for c in range(chunks):
        over(1, quads, lambda i: each_near(lambda j: q_relay(c, i, j).wait_send()))

    high = tout.shape[1]
    logs = [stat[place, :, :, pl.ds(0, high)]]
    for j in range(1, QUAD):
        t_send(j).wait_recv()
        logs.append(tin[j].T.reshape(quads, rows, high))
    top = functools.reduce(jnp.maximum, logs)
    parts = [jnp.exp(log - top) for log in logs]
    total = functools.reduce(jnp.add, parts)
    zstat[:, :, pl.ds(0, high)] = top + jnp.log(total)
    for j in range(QUAD):
        share[j, :, :, pl.ds(0, high)] = parts[j] / total
    over(1, quads, lambda i: y_send(i).start())
    ystat[0] = zstat[quad]

    def merged(h, i):
        g = next_quad(i)
        value = local[place, g, :, cols(h)] * share[0, g, :, pl.ds(h, 1)]
        for j in range(1, QUAD):
            value = value + decode(xin[j, i, :, cols(h)]) * share[j, g, :, pl.ds(h, 1)]
        return value

    for c in range(chunks):
        def cross(i):
            each_near(lambda j: x_send(c, j, i).wait_recv())
            for h in heads_of(c):
                zout[i, :, cols(h)] = encode(merged(h, i))
            z_send(c, i).start()
        over(1, quads, cross)
    each_near(lambda j: x_own(j).wait_recv())
    for h in range(heads):
        mine[:, cols(h)] = merged(h, 0)

    for c in range(chunks):
        over(1, quads, lambda i: each_near(lambda j: x_send(c, j, i).wait_send()))
    each_near(lambda j: x_own(j).wait_send())
    each_near(lambda j: t_send(j).wait_send())
    for c in range(chunks):
        over(1, quads, lambda i: z_send(c, i).wait_send())
    over(1, quads, lambda i: y_send(i).wait_send())
    over(1, quads, lambda i: y_send(i).wait_recv())
    logs = ystat[...]
    part = jnp.exp(logs - jnp.max(logs, axis=0, keepdims=True))
    ystat[...] = part / jnp.sum(part, axis=0, keepdims=True)
    for c in range(chunks):
        over(1, quads, lambda i: z_send(c, i).wait_recv())
        for h in heads_of(c):
            total = mine[:, cols(h)] * ystat[0, :, pl.ds(h, 1)]
            for i in range(1, quads):
                total = total + decode(zin[i, :, cols(h)]) * ystat[i, :, pl.ds(h, 1)]
            o_ref[:, cols(h)] = total.astype(o_ref.dtype)


def body(n, queries, keys, values):
    rows, columns = queries.shape
    depth = keys.shape[0]
    heads = columns // HEAD_DIM
    chunks = len(split_heads(heads))
    quads = n // QUAD
    high = 8 * pl.cdiv(heads, 8)
    dma = pltpu.SemaphoreType.DMA
    hbm = pl.BlockSpec(memory_space=pltpu.HBM)
    return pl.pallas_call(
        functools.partial(kernel, n),
        out_shape=jax.ShapeDtypeStruct((rows, columns), jnp.bfloat16),
        in_specs=[hbm, hbm, hbm],
        out_specs=pl.BlockSpec(memory_space=pltpu.VMEM),
        scratch_shapes=[
            pltpu.VMEM((QUAD, quads, rows, columns), jnp.bfloat16),
            pltpu.VMEM((heads, depth, HEAD_DIM), jnp.bfloat16),
            pltpu.VMEM((heads, depth, HEAD_DIM), jnp.bfloat16),
            pltpu.VMEM((QUAD, quads, rows, columns), jnp.float32),
            pltpu.VMEM((QUAD, quads, rows, LANES), jnp.float32),
            pltpu.VMEM((QUAD, quads, rows, columns), LINK),
            pltpu.VMEM((QUAD, quads, rows, columns), LINK),
            pltpu.VMEM((quads, rows, columns), LINK),
            pltpu.VMEM((quads, rows, columns), LINK),
            pltpu.VMEM((QUAD, high, quads * rows), jnp.float32),
            pltpu.VMEM((QUAD, high, quads * rows), jnp.float32),
            pltpu.VMEM((quads, rows, LANES), jnp.float32),
            pltpu.VMEM((quads, rows, LANES), jnp.float32),
            pltpu.VMEM((QUAD, quads, rows, LANES), jnp.float32),
            pltpu.VMEM((rows, columns), jnp.float32),
            dma, dma((heads,)), dma((heads,)),
            dma((QUAD,)), dma((QUAD,)),
            dma((heads, quads)), dma((heads, quads)),
            dma((chunks, quads, QUAD)), dma((chunks, quads, QUAD)),
            dma((chunks, QUAD, quads)), dma((chunks, QUAD, quads)),
            dma((QUAD,)), dma((QUAD,)), dma((QUAD,)), dma((QUAD,)),
            dma((chunks, quads)), dma((chunks, quads)),
            dma((quads,)), dma((quads,)),
        ],
        compiler_params=pltpu.CompilerParams(
            collective_id=0, has_side_effects=True, vmem_limit_bytes=56500000
        ),
        name="attend",
    )(queries, keys, values)


def solution(mesh):
    spec = P(("groups", "seq"), "tensor")
    return jax.shard_map(
        functools.partial(body, mesh.shape["seq"]),
        mesh=mesh,
        in_specs=(spec, spec, spec),
        out_specs=spec,
        check_vma=False,
    )
```
